512 devices in a mesh: section: 16 (over z, core), expert: 16 (over x_lo, y), dp: 2 (over x_hi).
Axes of the slice: x: 4 (x_hi: 2, x_lo: 2; x = x_hi * 2 + x_lo), y: 8, z: 8, core: 2. Of those that a mesh axis runs over, the one named last changes fastest.
Arguments:
- acts: bfloat16 [16, 4096, 1536], P('section', ('expert', 'dp')), may hold values from -6 to 6
- norm_gain: float32 [16, 1536], P('section'), may hold values from 0.1 to 1.9
- w_gate: bfloat16 [16, 1536, 6144], P('section', None, 'expert'), may hold values from -0.15625 to 0.15625
- w_up: bfloat16 [16, 1536, 6144], P('section', None, 'expert'), may hold values from -0.15625 to 0.15625
- w_down: bfloat16 [16, 6144, 1536], P('section', 'expert'), may hold values from -0.15625 to 0.15625
- routes: int32 [2, 16, 4096, 2], P(None, 'section', ('expert', 'dp')), may hold values from 0 to 3, all different within a row; in each aligned block of 128 rows (0 to 127, 128 to 255, ..., all dimensions but the last counted through in order) at most 66 rows name the same one
- gates: float32 [2, 16, 4096, 2], P(None, 'section', ('expert', 'dp')), may hold values from 0.2 to 1
Outputs:
- out: bfloat16 [16, 4096, 1536], P('section', ('expert', 'dp'))
The draws below stay inside these ranges and needn't reach their ends.
Inputs may be any that keep to these rules, and one draw needn't show every extreme that they name: `routes`: each row names 2 different experts. Within the rows of one device at one visit (aligned blocks of 128 rows) no expert is named by more than 66 rows, a bound that some block reaches.
All inputs are finite; a program needn't handle non-finite values.
Results may differ from the reference program's by a relative error of at most 0.0065.
Values may be sent and summed in bfloat16 or wider, within the bound.
A program may use at most 64 MiB of HBM per device.

```python
import math
import jax
import jax.numpy as jnp
import numpy as np
from jax import lax

D = 1536
FF = 1536
EXPERTS = 4
TOP = 2
STOPS = 2
TOK_DEV = 128
ROWS = 4096
CAP = 66
N_SECTION = 16
N_EXPERT = 16


def shard_levels(stream_key, dims, cuts, low, largest):
    loudness, own = 1.0, jax.random.fold_in(stream_key, 6)
    for position, shards_of in cuts:
        draws = jnp.exp(jax.random.uniform(jax.random.fold_in(own, position), (shards_of,), jnp.float32, low / len(cuts), largest / len(cuts)))
        loudness = loudness * jnp.repeat(draws, dims[position] // shards_of).reshape([-1 if axis == position else 1 for axis in range(len(dims))])
    return loudness


def routed_block(key, own, number, rows, amount, top, limit, slope):
    ranking = jax.random.permutation(key, amount)
    heavy_load, common = shares(amount, rows * top, limit, slope, True), shares(amount, rows * top, limit, slope, False)
    places = jnp.arange(amount)

    def named(tallies, rotation):
        used = int((tallies > 0).sum())
        fixed = max(1, used // 4)
        shifted = fixed + (places - fixed + rotation * (used - fixed)) % max(1, amount - fixed)
        return jnp.zeros((amount,), jnp.int32).at[ranking[jnp.where(places < fixed, places, shifted)]].set(jnp.asarray(tallies, jnp.int32))

    tallies = jnp.where(number % 4 == 0, named(heavy_load, number // 4), named(common, number - number // 4 - 1))
    mixed = jax.random.permutation(jax.random.fold_in(own, 3), amount)
    source_of, receiver = mixed[0:amount // 2 * 2:2], mixed[1:amount // 2 * 2:2]
    room = jnp.minimum(tallies[source_of] - 1, limit - tallies[receiver]) // 2
    room = jnp.where((source_of == ranking[0]) | (receiver == ranking[0]) | (tallies[receiver] == 0), 0, jnp.maximum(room, 0))
    shifted = jax.random.randint(jax.random.fold_in(own, 4), (amount // 2,), 0, 1 << 20) % (room + 1)
    tallies = tallies.at[source_of].add(-shifted).at[receiver].add(shifted)
    labels = jnp.searchsorted(jnp.cumsum(tallies), jnp.arange(rows * top), side="right").astype(jnp.int32)
    listing = labels.reshape(top, rows).T
    listing = listing[jax.random.permutation(jax.random.fold_in(own, 1), rows)]
    rotation = jax.random.randint(jax.random.fold_in(own, 2), (rows, 1), 0, top)
    return jnp.take_along_axis(listing, (jnp.arange(top)[None, :] + rotation) % top, axis=1)


def shares(amount, total, limit, slope, full):
    portions = [(1 << 20) // math.isqrt(standing ** slope) + 1 for standing in range(1, amount + 1)]
    largest = limit if full else min(limit, max(-(-total // amount), total * portions[0] // sum(portions)))
    least = 1 if total - largest >= amount - 1 else 0
    holding, surplus = [largest] + [least] * (amount - 1), total - largest - least * (amount - 1)
    while surplus > 0:
        movable = [i for i in range(1, amount) if holding[i] < largest] or [i for i in range(1, amount) if holding[i] < limit]
        pool, left = sum([portions[i] for i in movable]), surplus
        for i in movable:
            more = min(limit - holding[i], max(1, left * portions[i] // pool), surplus)
            holding[i] = holding[i] + more
            surplus = surplus - more
    return np.array(holding)


def gaussian(stream_key, extent, width, limit, split=(), held_as=jnp.bfloat16):
    array = width * jax.random.normal(stream_key, extent, jnp.float32)
    if split:
        array = array * shard_levels(stream_key, extent, split, -0.22, 0.18)
    return jnp.clip(array, -limit, limit).astype(held_as)


def setup_inputs(seed: int = 0) -> dict:
    streams_of = jax.random.split(jax.random.key(seed), 8)
    acts = gaussian(streams_of[0], (N_SECTION, ROWS, D), 1.0, 6.0, ((0, 16), (1, 32)))
    norm_gain = jnp.clip(1.0 + 0.18 * jax.random.normal(streams_of[1], (N_SECTION, D), jnp.float32), 0.1, 1.9)
    w_gate = gaussian(streams_of[2], (N_SECTION, D, EXPERTS * FF), D ** -0.5, 0.15625, ((0, 16), (2, 16)))
    w_up = gaussian(streams_of[3], (N_SECTION, D, EXPERTS * FF), D ** -0.5, 0.15625, ((0, 16), (2, 16)))
    w_down = gaussian(streams_of[4], (N_SECTION, EXPERTS * FF, D), FF ** -0.5, 0.15625, ((0, 16), (1, 16)))
    routes_keys = jax.random.split(jax.random.fold_in(streams_of[5], 1), STOPS * N_SECTION * ROWS // TOK_DEV)
    routes_turns = jax.random.permutation(jax.random.fold_in(streams_of[5], 3), STOPS * N_SECTION * ROWS // TOK_DEV)
    routes = jax.vmap(lambda own, number: routed_block(jax.random.fold_in(streams_of[5], 2), own, number, TOK_DEV, EXPERTS, TOP, CAP, 2))(routes_keys, routes_turns).reshape((STOPS, N_SECTION, ROWS, TOP))
    gates = jnp.clip(jnp.exp(math.log(1.0) - 1.609438 * jax.random.uniform(streams_of[6], (STOPS, N_SECTION, ROWS, TOP), jnp.float32) ** shard_levels(streams_of[6], (STOPS, N_SECTION, ROWS, TOP), ((1, 16), (2, 32)), -0.2, 0.2)), 0.2, 1.0)
    return {"acts": acts, "norm_gain": norm_gain, "w_gate": w_gate, "w_up": w_up, "w_down": w_down, "routes": routes, "gates": gates}


epsilon = 1e-05

def expert_rows(packed):
    flat_rows, gate_cols, up_cols, down_rows = packed
    gate_pre = jnp.dot(flat_rows, gate_cols, preferred_element_type=jnp.float32)
    up_pre = jnp.dot(flat_rows, up_cols, preferred_element_type=jnp.float32)
    hidden = (jax.nn.silu(gate_pre) * up_pre).astype(jnp.bfloat16)
    slab_count = N_EXPERT // EXPERTS
    slab_width = FF // slab_count
    total = jnp.zeros((flat_rows.shape[0], D), jnp.float32)
    for slab_index in range(slab_count):
        lower = slab_index * slab_width
        upper = lower + slab_width
        part = jnp.dot(hidden[:, lower:upper], down_rows[lower:upper], preferred_element_type=jnp.float32)
        total = total + lax.optimization_barrier(part.astype(jnp.bfloat16)).astype(jnp.float32)
    return total

def section_step(packed):
    moved, gain_row, gate_all, up_all, down_all, route_rows, gate_rows = packed
    widened = moved.astype(jnp.float32)
    scale_row = lax.rsqrt(lax.optimization_barrier(jnp.mean(widened * widened, axis=-1, keepdims=True)) + epsilon)
    normed = (widened * scale_row * gain_row.astype(jnp.float32)).astype(jnp.bfloat16)
    flat_route = route_rows.reshape(-1).astype(jnp.int32)
    onehot = (flat_route[:, None] == jnp.arange(EXPERTS, dtype=jnp.int32)[None, :]).astype(jnp.int32)
    before = (jnp.cumsum(onehot, axis=0).astype(jnp.int32) - onehot) * onehot
    slot_of = lax.optimization_barrier(jnp.sum(before, axis=1)).astype(jnp.int32)
    room = ROWS // TOK_DEV * CAP
    repeated = jnp.repeat(normed, TOP, axis=0)
    buffers = jnp.zeros((EXPERTS, room, D), jnp.bfloat16).at[flat_route, slot_of].set(repeated)
    gate_split = gate_all.reshape(D, EXPERTS, FF).transpose(1, 0, 2)
    up_split = up_all.reshape(D, EXPERTS, FF).transpose(1, 0, 2)
    down_split = down_all.reshape(EXPERTS, FF, D)
    results = lax.map(expert_rows, (buffers, gate_split, up_split, down_split))
    picked = results[flat_route, slot_of].reshape(-1, TOP, D)
    mixture = lax.optimization_barrier(jnp.sum(picked * gate_rows.astype(jnp.float32)[..., None], axis=1))
    return (widened + mixture).astype(jnp.bfloat16)

def reference(acts, norm_gain, w_gate, w_up, w_down, routes, gates):
    current = acts
    for stop_index in range(STOPS):
        current = jnp.roll(current, 1, axis=0)
        current = lax.map(section_step, (current, norm_gain, w_gate, w_up, w_down, routes[stop_index], gates[stop_index]))
    return current
```

```python
import jax
import jax.numpy as jnp
from jax import lax
from jax.sharding import PartitionSpec as P

D = 1536
EXPERTS = 4
STOPS = 2

epsilon = 1e-05


def passed_along(block, axis, distance):
    devices = range(lax.axis_size(axis))
    route = [((i - distance) % len(devices), i) for i in devices]
    return lax.ppermute(block, axis, route)


def body(acts, norm_gain, w_gate, w_up, w_down, routes, gates):
    slab_count = lax.axis_size("expert") // EXPERTS
    mine = lax.axis_index("expert") // slab_count
    gain_row = norm_gain[0]
    gate_cols = w_gate[0]
    up_cols = w_up[0]
    down_rows = w_down[0]
    current = acts[0]
    dense = jnp.sum(
        jnp.where(
            routes[:, 0, :, :, None] == jnp.arange(EXPERTS, dtype=jnp.int32),
            gates[:, 0, :, :, None],
            0.0,
        ),
        axis=2,
    )
    every = lax.all_gather(dense, "expert", axis=1, tiled=True)
    column = jnp.sum(
        jnp.where(jnp.arange(EXPERTS, dtype=jnp.int32) == mine, every, 0.0), axis=2, keepdims=True
    )
    for stop_index in range(STOPS):
        current = passed_along(current, "section", 1)
        widened = current.astype(jnp.float32)
        scale_row = lax.rsqrt(jnp.mean(widened * widened, axis=-1, keepdims=True) + epsilon)
        normed = (widened * scale_row * gain_row).astype(jnp.bfloat16)
        rows = lax.all_gather(normed, "expert", axis=0, tiled=True)
        gate_pre = jnp.dot(rows, gate_cols, preferred_element_type=jnp.float32)
        up_pre = jnp.dot(rows, up_cols, preferred_element_type=jnp.float32)
        hidden = (jax.nn.silu(gate_pre) * up_pre).astype(jnp.bfloat16)
        partial_value = jnp.dot(hidden, down_rows, preferred_element_type=jnp.float32)
        weighted = (partial_value * column[stop_index]).astype(jnp.bfloat16)
        mixture = lax.psum_scatter(weighted, "expert", scatter_dimension=0, tiled=True)
        current = (widened + mixture.astype(jnp.float32)).astype(jnp.bfloat16)
    return current[None]


def solution(mesh):
    placed = (
        P("section", ("expert", "dp"), None),
        P("section", None),
        P("section", None, "expert"),
        P("section", None, "expert"),
        P("section", "expert", None),
        P(None, "section", ("expert", "dp"), None),
        P(None, "section", ("expert", "dp"), None),
    )
    return jax.shard_map(
        body,
        mesh=mesh,
        in_specs=placed,
        out_specs=P("section", ("expert", "dp"), None),
        check_vma=False,
    )
```

```python
import jax
import jax.numpy as jnp
import numpy as np
from jax import lax
from jax.experimental import pallas as pl
from jax.experimental.pallas import tpu as pltpu
from jax.sharding import PartitionSpec as P

D = 1536
EXPERTS = 4
STOPS = 2
RING = 8
HALF = 64

epsilon = 1e-05

FLOWS = (
    ("a", 1, 4, 0),
    ("a", -1, 3, 0),
    ("a", 1, 3, 1),
    ("a", -1, 4, 1),
    ("b", 1, 4, 0),
    ("b", -1, 3, 0),
)
B_FLOWS = (4, 5)

SLOT = {"a0": 0, "an0": 1, "b0": 2, "bx0": 3}
SOURCE = [(0, 0, 0), (1, 0, 0), (0, 0, 1), (1, 0, 1)]
GROUPS = [(0, 1)]
for _k in range(1, 5):
    _first = len(SOURCE)
    for _f, (_b, _s, _n, _o) in enumerate(FLOWS):
        if _k <= _n:
            SLOT[(_f, _k)] = len(SOURCE)
            SOURCE.append((_o, _s * _k, int(_b == "b")))
    for _f in B_FLOWS:
        if _k <= FLOWS[_f][2]:
            SLOT[("x", _f, _k)] = len(SOURCE)
            SOURCE.append((1, FLOWS[_f][1] * _k, 1))
    GROUPS.append((_first // 4, len(SOURCE) // 4))
SLOTS = len(SOURCE)

BACK = {}
for _f, _flow in enumerate(FLOWS):
    for _k in range(_flow[2]):
        BACK[(_f, _k)] = len(BACK)
for _f in B_FLOWS:
    for _k in range(1, FLOWS[_f][2] + 1):
        BACK[("x", _f, _k)] = len(BACK)
BACK["bx0"] = len(BACK)
BACK["ax0"] = len(BACK)
BACKS = len(BACK)


def visit_kernel(
    x_ref, col_ref, wg_ref, wu_ref, wd_ref, out_ref,
    rows, part, stage, back, send_sem, recv_sem, bsend_sem, brecv_sem,
):
    me = lax.axis_index("expert")
    ring = me // RING
    y = me % RING
    turn = 1 - 2 * (lax.axis_index("section") % 2)
    ahead = ring * RING + (y + turn + RING) % RING
    behind = ring * RING + (y - turn + RING) % RING
    across = (1 - ring) * RING + y

    barrier = pltpu.get_barrier_semaphore()
    for peer in (ahead, behind, across):
        pl.semaphore_signal(
            barrier, inc=1, device_id={"expert": peer}, device_id_type=pl.DeviceIdType.MESH
        )
    pl.semaphore_wait(barrier, 3)

    own = {"a": x_ref.at[pl.ds(0, HALF)], "b": x_ref.at[pl.ds(HALF, HALF)]}
    sent = []

    def send(source, slot, peer):
        copy = pltpu.make_async_remote_copy(
            src_ref=source,
            dst_ref=rows.at[slot],
            send_sem=send_sem.at[slot],
            recv_sem=recv_sem.at[slot],
            device_id={"expert": peer},
            device_id_type=pl.DeviceIdType.MESH,
        )
        copy.start()
        sent.append(copy)
        return copy

    def give(slot, place, peer):
        copy = pltpu.make_async_remote_copy(
            src_ref=stage.at[slot],
            dst_ref=back.at[place],
            send_sem=bsend_sem.at[place],
            recv_sem=brecv_sem.at[place],
            device_id={"expert": peer},
            device_id_type=pl.DeviceIdType.MESH,
        )
        copy.start()
        sent.append(copy)
        return copy

    def compute(group):
        def chunk(c, carry):
            x = rows[pl.ds(c * 4, 4)].reshape(4 * HALF, D)
            g = jnp.dot(x, wg_ref[...], preferred_element_type=jnp.float32)
            u = jnp.dot(x, wu_ref[...], preferred_element_type=jnp.float32)
            h = (g / (1.0 + jnp.exp(-g)) * u).astype(jnp.bfloat16)
            p = jnp.dot(h, wd_ref[...], preferred_element_type=jnp.float32)
            w = col_ref[pl.ds(c * 4, 4)].reshape(4 * HALF, 1)
            part[pl.ds(c * 4, 4)] = (p * w).reshape(4, HALF, D)
            return carry

        lax.fori_loop(GROUPS[group][0], GROUPS[group][1], chunk, 0)

    flight = {}
    home = {}

    def across_back(slot, place):
        stage[slot] = part[slot].astype(jnp.bfloat16)
        home[place] = give(slot, BACK[place], across)

    flight["an0"] = send(own["a"], SLOT["an0"], across)
    for f in (0, 1, 4, 5):
        block, sign, _, _ = FLOWS[f]
        flight[(f, 1)] = send(own[block], SLOT[(f, 1)], ahead if sign > 0 else behind)
    flight["bx0"] = send(own["b"], SLOT["bx0"], across)
    rows[SLOT["a0"]] = x_ref[pl.ds(0, HALF)]
    rows[SLOT["b0"]] = x_ref[pl.ds(HALF, HALF)]
    flight["an0"].wait_recv()
    for f in (2, 3):
        flight[(f, 1)] = send(
            rows.at[SLOT["an0"]], SLOT[(f, 1)], ahead if FLOWS[f][1] > 0 else behind
        )
    flight["bx0"].wait_recv()
    compute(0)
    across_back(SLOT["bx0"], "bx0")
    for k in range(1, 5):
        for f in (4, 5, 0, 1, 2, 3):
            _, sign, hops, _ = FLOWS[f]
            if k > hops:
                continue
            flight[(f, k)].wait_recv()
            if k < hops:
                flight[(f, k + 1)] = send(
                    rows.at[SLOT[(f, k)]], SLOT[(f, k + 1)], ahead if sign > 0 else behind
                )
            if f in B_FLOWS:
                flight[("x", f, k)] = send(rows.at[SLOT[(f, k)]], SLOT[("x", f, k)], across)
        for f in B_FLOWS:
            if k <= FLOWS[f][2]:
                flight[("x", f, k)].wait_recv()
        compute(k)
        for f in B_FLOWS:
            if k <= FLOWS[f][2]:
                across_back(SLOT[("x", f, k)], ("x", f, k))

    for k in range(4, 0, -1):
        order = (1, 2, 0, 3, 5, 4) if k == 3 else (0, 3, 1, 2, 4, 5)
        for f in order:
            _, sign, hops, _ = FLOWS[f]
            if k > hops:
                continue
            total = part[SLOT[(f, k)]]
            if f in B_FLOWS:
                home[("x", f, k)].wait_recv()
                total = total + back[BACK[("x", f, k)]].astype(jnp.float32)
            if k < hops:
                home[(f, k)].wait_recv()
                total = total + back[BACK[(f, k)]].astype(jnp.float32)
            stage[SLOT[(f, k)]] = total.astype(jnp.bfloat16)
            home[(f, k - 1)] = give(
                SLOT[(f, k)], BACK[(f, k - 1)], behind if sign > 0 else ahead
            )

    def gathered(slot, places):
        total = part[slot]
        for place in places:
            home[place].wait_recv()
            total = total + back[BACK[place]].astype(jnp.float32)
        return total

    stage[SLOT["an0"]] = gathered(SLOT["an0"], [(2, 0), (3, 0)]).astype(jnp.bfloat16)
    home["ax0"] = give(SLOT["an0"], BACK["ax0"], across)
    out_ref[pl.ds(HALF, HALF)] = gathered(SLOT["b0"], ["bx0", (4, 0), (5, 0)])
    out_ref[pl.ds(0, HALF)] = gathered(SLOT["a0"], [(0, 0), (1, 0), "ax0"])
    for copy in sent:
        copy.wait_send()


def visit(normed, col, wg, wu, wd):
    vmem = pl.BlockSpec(memory_space=pltpu.VMEM)
    return pl.pallas_call(
        visit_kernel,
        out_shape=jax.ShapeDtypeStruct((2 * HALF, D), jnp.float32),
        in_specs=[vmem] * 5,
        out_specs=vmem,
        scratch_shapes=[
            pltpu.VMEM((SLOTS, HALF, D), jnp.bfloat16),
            pltpu.VMEM((SLOTS, HALF, D), jnp.float32),
            pltpu.VMEM((SLOTS, HALF, D), jnp.bfloat16),
            pltpu.VMEM((BACKS, HALF, D), jnp.bfloat16),
            pltpu.SemaphoreType.DMA((SLOTS,)),
            pltpu.SemaphoreType.DMA((SLOTS,)),
            pltpu.SemaphoreType.DMA((BACKS,)),
            pltpu.SemaphoreType.DMA((BACKS,)),
        ],
        compiler_params=pltpu.CompilerParams(
            collective_id=0, has_side_effects=True, vmem_limit_bytes=60 * 1024 * 1024
        ),
    )(normed, col, wg, wu, wd)


def passed_along(block, axis, distance):
    devices = range(lax.axis_size(axis))
    route = [((i - distance) % len(devices), i) for i in devices]
    return lax.ppermute(block, axis, route)


def body(acts, norm_gain, w_gate, w_up, w_down, routes, gates):
    me = lax.axis_index("expert")
    mine = me // (lax.axis_size("expert") // EXPERTS)
    gain_row = norm_gain[0]
    current = acts[0]
    experts = jnp.arange(EXPERTS, dtype=jnp.int32)
    dense = jnp.sum(
        jnp.where(routes[:, 0, :, :, None] == experts, gates[:, 0, :, :, None], 0.0), axis=2
    )
    every = lax.all_gather(dense, "expert", axis=1, tiled=True)
    column = jnp.sum(jnp.where(experts == mine, every, 0.0), axis=2)
    table = np.array(SOURCE, dtype=np.int32)
    turn = 1 - 2 * (lax.axis_index("section") % 2)
    source = (me // RING + table[:, 0]) % 2 * RING + (me % RING - turn * table[:, 1] + RING) % RING
    column = column.reshape(STOPS, 4 * RING, HALF)
    column = jnp.take(column, source * 2 + table[:, 2], axis=1)[..., None]
    for stop_index in range(STOPS):
        current = passed_along(current, "section", 1)
        widened = current.astype(jnp.float32)
        scale_row = lax.rsqrt(jnp.mean(widened * widened, axis=-1, keepdims=True) + epsilon)
        normed = (widened * scale_row * gain_row).astype(jnp.bfloat16)
        mixture = visit(normed, column[stop_index], w_gate[0], w_up[0], w_down[0])
        current = (widened + mixture).astype(jnp.bfloat16)
    return current[None]


def solution(mesh):
    placed = (
        P("section", ("expert", "dp"), None),
        P("section", None),
        P("section", None, "expert"),
        P("section", None, "expert"),
        P("section", "expert", None),
        P(None, "section", ("expert", "dp"), None),
        P(None, "section", ("expert", "dp"), None),
    )
    return jax.shard_map(
        body,
        mesh=mesh,
        in_specs=placed,
        out_specs=P("section", ("expert", "dp"), None),
        check_vma=False,
    )
```

```python
import jax
import jax.numpy as jnp
import numpy as np
from jax import lax
from jax.experimental import pallas as pl
from jax.experimental.pallas import tpu as pltpu
from jax.sharding import PartitionSpec as P

D = 1536
EXPERTS = 4
STOPS = 2
RING = 8
HALF = 64

epsilon = 1e-05

FLOWS = (
    ("a", 1, 4, 0),
    ("a", -1, 3, 0),
    ("a", 1, 3, 1),
    ("a", -1, 4, 1),
    ("b", 1, 4, 0),
    ("b", -1, 3, 0),
)
B_FLOWS = (4, 5)

SLOT = {"a0": 0, "an0": 1, "b0": 2, "bx0": 3}
SOURCE = [(0, 0, 0), (1, 0, 0), (0, 0, 1), (1, 0, 1)]
GROUPS = [(0, 1)]
for _k in range(1, 5):
    _first = len(SOURCE)
    for _f, (_b, _s, _n, _o) in enumerate(FLOWS):
        if _k <= _n:
            SLOT[(_f, _k)] = len(SOURCE)
            SOURCE.append((_o, _s * _k, int(_b == "b")))
    for _f in B_FLOWS:
        if _k <= FLOWS[_f][2]:
            SLOT[("x", _f, _k)] = len(SOURCE)
            SOURCE.append((1, FLOWS[_f][1] * _k, 1))
    GROUPS.append((_first // 4, len(SOURCE) // 4))
SLOTS = len(SOURCE)

BACK = {}
for _f, _flow in enumerate(FLOWS):
    for _k in range(_flow[2]):
        BACK[(_f, _k)] = len(BACK)
for _f in B_FLOWS:
    for _k in range(1, FLOWS[_f][2] + 1):
        BACK[("x", _f, _k)] = len(BACK)
BACK["bx0"] = len(BACK)
BACK["ax0"] = len(BACK)
BACKS = len(BACK)


def visit_kernel(
    x_ref, col_ref, wg_ref, wu_ref, wd_ref, out_ref,
    rows, part, stage, back, send_sem, recv_sem, bsend_sem, brecv_sem,
):
    me = lax.axis_index("expert")
    ring = me // RING
    y = me % RING
    turn = 1 - 2 * (lax.axis_index("section") % 2)
    ahead = ring * RING + (y + turn + RING) % RING
    behind = ring * RING + (y - turn + RING) % RING
    across = (1 - ring) * RING + y

    barrier = pltpu.get_barrier_semaphore()
    for peer in (ahead, behind, across):
        pl.semaphore_signal(
            barrier, inc=1, device_id={"expert": peer}, device_id_type=pl.DeviceIdType.MESH
        )
    pl.semaphore_wait(barrier, 3)

    own = {"a": x_ref.at[pl.ds(0, HALF)], "b": x_ref.at[pl.ds(HALF, HALF)]}
    sent = []

    def send(source, slot, peer):
        copy = pltpu.make_async_remote_copy(
            src_ref=source,
            dst_ref=rows.at[slot],
            send_sem=send_sem.at[slot],
            recv_sem=recv_sem.at[slot],
            device_id={"expert": peer},
            device_id_type=pl.DeviceIdType.MESH,
        )
        copy.start()
        sent.append(copy)
        return copy

    def give(slot, place, peer):
        copy = pltpu.make_async_remote_copy(
            src_ref=stage.at[slot],
            dst_ref=back.at[place],
            send_sem=bsend_sem.at[place],
            recv_sem=brecv_sem.at[place],
            device_id={"expert": peer},
            device_id_type=pl.DeviceIdType.MESH,
        )
        copy.start()
        sent.append(copy)
        return copy

    def compute(c):
        def chunk(i, carry):
            x = rows[pl.ds(i * 4, 4)].reshape(4 * HALF, D)
            g = jnp.dot(x, wg_ref[...], preferred_element_type=jnp.float32)
            u = jnp.dot(x, wu_ref[...], preferred_element_type=jnp.float32)
            h = (g / (1.0 + jnp.exp(-g)) * u).astype(jnp.bfloat16)
            p = jnp.dot(h, wd_ref[...], preferred_element_type=jnp.float32)
            w = col_ref[pl.ds(i * 4, 4)].reshape(4 * HALF, 1)
            part[pl.ds(i * 4, 4)] = (p * w).reshape(4, HALF, D)
            return carry

        lax.fori_loop(c, c + 1, chunk, 0)

    flight = {}
    home = {}

    def across_back(slot, place):
        stage[slot] = part[slot].astype(jnp.bfloat16)
        home[place] = give(slot, BACK[place], across)

    flight["an0"] = send(own["a"], SLOT["an0"], across)
    for f in (0, 1, 4, 5):
        block, sign, _, _ = FLOWS[f]
        flight[(f, 1)] = send(own[block], SLOT[(f, 1)], ahead if sign > 0 else behind)
    flight["bx0"] = send(own["b"], SLOT["bx0"], across)
    rows[SLOT["a0"]] = x_ref[pl.ds(0, HALF)]
    rows[SLOT["b0"]] = x_ref[pl.ds(HALF, HALF)]
    flight["an0"].wait_recv()
    for f in (2, 3):
        flight[(f, 1)] = send(
            rows.at[SLOT["an0"]], SLOT[(f, 1)], ahead if FLOWS[f][1] > 0 else behind
        )
    def returned(f, k):
        _, sign, hops, _ = FLOWS[f]
        total = part[SLOT[(f, k)]]
        if f in B_FLOWS:
            home[("x", f, k)].wait_recv()
            total = total + back[BACK[("x", f, k)]].astype(jnp.float32)
        if k < hops:
            home[(f, k)].wait_recv()
            total = total + back[BACK[(f, k)]].astype(jnp.float32)
        stage[SLOT[(f, k)]] = total.astype(jnp.bfloat16)
        home[(f, k - 1)] = give(SLOT[(f, k)], BACK[(f, k - 1)], behind if sign > 0 else ahead)

    for k in range(1, 5):
        waiting = list(range(*GROUPS[k - 1]))
        for pair in ((4, 5), (0, 1), (2, 3)):
            for f in pair:
                _, sign, hops, _ = FLOWS[f]
                if k > hops:
                    continue
                flight[(f, k)].wait_recv()
                if k < hops:
                    flight[(f, k + 1)] = send(
                        rows.at[SLOT[(f, k)]], SLOT[(f, k + 1)], ahead if sign > 0 else behind
                    )
                if f in B_FLOWS:
                    flight[("x", f, k)] = send(rows.at[SLOT[(f, k)]], SLOT[("x", f, k)], across)
            if waiting and pair != (2, 3):
                if k == 1:
                    flight["bx0"].wait_recv()
                else:
                    for f in B_FLOWS:
                        if pair == (4, 5):
                            flight[("x", f, k - 1)].wait_recv()
                compute(waiting.pop(0))
    for f in B_FLOWS:
        across_back(SLOT[("x", f, 3)], ("x", f, 3))
    returned(1, 3)
    returned(2, 3)
    flight[("x", 4, 4)].wait_recv()
    compute(GROUPS[4][0])
    across_back(SLOT[("x", 4, 4)], ("x", 4, 4))
    returned(0, 4)
    returned(3, 4)
    returned(5, 3)
    for k in (2, 1):
        for f in B_FLOWS:
            across_back(SLOT[("x", f, k)], ("x", f, k))
    across_back(SLOT["bx0"], "bx0")

    returned(4, 4)
    for f in (0, 3, 4):
        returned(f, 3)
    for k in (2, 1):
        for f in (1, 2, 5, 0, 3, 4):
            returned(f, k)

    def gathered(slot, places):
        total = part[slot]
        for place in places:
            home[place].wait_recv()
            total = total + back[BACK[place]].astype(jnp.float32)
        return total

    stage[SLOT["an0"]] = gathered(SLOT["an0"], [(2, 0), (3, 0)]).astype(jnp.bfloat16)
    home["ax0"] = give(SLOT["an0"], BACK["ax0"], across)
    out_ref[pl.ds(HALF, HALF)] = gathered(SLOT["b0"], ["bx0", (4, 0), (5, 0)])
    out_ref[pl.ds(0, HALF)] = gathered(SLOT["a0"], [(0, 0), (1, 0), "ax0"])
    for copy in sent:
        copy.wait_send()


def visit(normed, col, wg, wu, wd):
    vmem = pl.BlockSpec(memory_space=pltpu.VMEM)
    return pl.pallas_call(
        visit_kernel,
        out_shape=jax.ShapeDtypeStruct((2 * HALF, D), jnp.float32),
        in_specs=[vmem] * 5,
        out_specs=vmem,
        scratch_shapes=[
            pltpu.VMEM((SLOTS, HALF, D), jnp.bfloat16),
            pltpu.VMEM((SLOTS, HALF, D), jnp.float32),
            pltpu.VMEM((SLOTS, HALF, D), jnp.bfloat16),
            pltpu.VMEM((BACKS, HALF, D), jnp.bfloat16),
            pltpu.SemaphoreType.DMA((SLOTS,)),
            pltpu.SemaphoreType.DMA((SLOTS,)),
            pltpu.SemaphoreType.DMA((BACKS,)),
            pltpu.SemaphoreType.DMA((BACKS,)),
        ],
        compiler_params=pltpu.CompilerParams(
            collective_id=0, has_side_effects=True, vmem_limit_bytes=60 * 1024 * 1024
        ),
    )(normed, col, wg, wu, wd)


def passed_along(block, axis, distance):
    devices = range(lax.axis_size(axis))
    route = [((i - distance) % len(devices), i) for i in devices]
    return lax.ppermute(block, axis, route)


def body(acts, norm_gain, w_gate, w_up, w_down, routes, gates):
    me = lax.axis_index("expert")
    gain_row = norm_gain[0]
    current = acts[0]
    named = jnp.arange(4 * EXPERTS, dtype=jnp.int32)[:, None, None, None] // EXPERTS
    dense = jnp.sum(jnp.where(routes[None, :, 0] == named, gates[None, :, 0], 0.0), axis=3)
    column = lax.all_to_all(dense, "expert", split_axis=0, concat_axis=0, tiled=True)
    table = np.array(SOURCE, dtype=np.int32)
    turn = 1 - 2 * (lax.axis_index("section") % 2)
    source = (me // RING + table[:, 0]) % 2 * RING + (me % RING - turn * table[:, 1] + RING) % RING
    column = column.reshape(2 * RING, STOPS, 2, HALF).transpose(1, 0, 2, 3)
    column = column.reshape(STOPS, 4 * RING, HALF)
    column = jnp.take(column, source * 2 + table[:, 2], axis=1)[..., None]
    for stop_index in range(STOPS):
        current = passed_along(current, "section", 1)
        widened = current.astype(jnp.float32)
        scale_row = lax.rsqrt(jnp.mean(widened * widened, axis=-1, keepdims=True) + epsilon)
        normed = (widened * scale_row * gain_row).astype(jnp.bfloat16)
        mixture = visit(normed, column[stop_index], w_gate[0], w_up[0], w_down[0])
        current = (widened + mixture).astype(jnp.bfloat16)
    return current[None]


def solution(mesh):
    placed = (
        P("section", ("expert", "dp"), None),
        P("section", None),
        P("section", None, "expert"),
        P("section", None, "expert"),
        P("section", "expert", None),
        P(None, "section", ("expert", "dp"), None),
        P(None, "section", ("expert", "dp"), None),
    )
    return jax.shard_map(
        body,
        mesh=mesh,
        in_specs=placed,
        out_specs=P("section", ("expert", "dp"), None),
        check_vma=False,
    )
```

```python
import jax
import jax.numpy as jnp
import numpy as np
from jax import lax
from jax.experimental import pallas as pl
from jax.experimental.pallas import tpu as pltpu
from jax.sharding import PartitionSpec as P

D = 1536
EXPERTS = 4
STOPS = 2
RING = 8
HALF = 64

epsilon = 1e-05

FLOWS = (
    ("a", 1, 4, 0),
    ("a", -1, 3, 0),
    ("a", 1, 3, 1),
    ("a", -1, 4, 1),
    ("b", 1, 4, 0),
    ("b", -1, 3, 0),
)
B_FLOWS = (4, 5)

SLOT = {"a0": 0, "an0": 1, "b0": 2, "bx0": 3}
SOURCE = [(0, 0, 0), (1, 0, 0), (0, 0, 1), (1, 0, 1)]
GROUPS = [(0, 1)]
for _k in range(1, 5):
    _first = len(SOURCE)
    for _f, (_b, _s, _n, _o) in enumerate(FLOWS):
        if _k <= _n:
            SLOT[(_f, _k)] = len(SOURCE)
            SOURCE.append((_o, _s * _k, int(_b == "b")))
    for _f in B_FLOWS:
        if _k <= FLOWS[_f][2]:
            SLOT[("x", _f, _k)] = len(SOURCE)
            SOURCE.append((1, FLOWS[_f][1] * _k, 1))
    GROUPS.append((_first // 4, len(SOURCE) // 4))
SLOTS = len(SOURCE)

BACK = {}
for _f, _flow in enumerate(FLOWS):
    for _k in range(_flow[2]):
        BACK[(_f, _k)] = len(BACK)
for _f in B_FLOWS:
    for _k in range(1, FLOWS[_f][2] + 1):
        BACK[("x", _f, _k)] = len(BACK)
BACK["bx0"] = len(BACK)
BACK["ax0"] = len(BACK)
BACKS = len(BACK)


def visit_kernel(
    x_ref, col_ref, wg_ref, wu_ref, wd_ref, out_ref,
    rows, part, stage, back, send_sem, recv_sem, bsend_sem, brecv_sem,
):
    me = lax.axis_index("expert")
    ring = me // RING
    y = me % RING
    turn = 1 - 2 * (lax.axis_index("section") % 2)
    ahead = ring * RING + (y + turn + RING) % RING
    behind = ring * RING + (y - turn + RING) % RING
    across = (1 - ring) * RING + y

    barrier = pltpu.get_barrier_semaphore()
    for peer in (ahead, behind, across):
        pl.semaphore_signal(
            barrier, inc=1, device_id={"expert": peer}, device_id_type=pl.DeviceIdType.MESH
        )
    pl.semaphore_wait(barrier, 3)

    own = {"a": x_ref.at[pl.ds(0, HALF)], "b": x_ref.at[pl.ds(HALF, HALF)]}
    sent = []

    def send(source, slot, peer):
        copy = pltpu.make_async_remote_copy(
            src_ref=source,
            dst_ref=rows.at[slot],
            send_sem=send_sem.at[slot],
            recv_sem=recv_sem.at[slot],
            device_id={"expert": peer},
            device_id_type=pl.DeviceIdType.MESH,
        )
        copy.start()
        sent.append(copy)
        return copy

    def give(slot, place, peer):
        copy = pltpu.make_async_remote_copy(
            src_ref=stage.at[slot],
            dst_ref=back.at[place],
            send_sem=bsend_sem.at[place],
            recv_sem=brecv_sem.at[place],
            device_id={"expert": peer},
            device_id_type=pl.DeviceIdType.MESH,
        )
        copy.start()
        sent.append(copy)
        return copy

    def compute(c):
        def chunk(i, carry):
            x = rows[pl.ds(i * 4, 4)].reshape(4 * HALF, D)
            g = jnp.dot(x, wg_ref[...], preferred_element_type=jnp.float32)
            u = jnp.dot(x, wu_ref[...], preferred_element_type=jnp.float32)
            h = (g / (1.0 + jnp.exp(-g)) * u).astype(jnp.bfloat16)
            p = jnp.dot(h, wd_ref[...], preferred_element_type=jnp.float32)
            w = col_ref[pl.ds(i * 4, 4)].reshape(4 * HALF, 1)
            part[pl.ds(i * 4, 4)] = (p * w).reshape(4, HALF, D)
            return carry

        lax.fori_loop(c, c + 1, chunk, 0)

    flight = {}
    home = {}

    def across_back(slot, place):
        stage[slot] = part[slot].astype(jnp.bfloat16)
        home[place] = give(slot, BACK[place], across)

    flight["an0"] = send(own["a"], SLOT["an0"], across)
    for f in (4, 5, 0, 1):
        block, sign, _, _ = FLOWS[f]
        flight[(f, 1)] = send(own[block], SLOT[(f, 1)], ahead if sign > 0 else behind)
    flight["bx0"] = send(own["b"], SLOT["bx0"], across)
    rows[SLOT["a0"]] = x_ref[pl.ds(0, HALF)]
    rows[SLOT["b0"]] = x_ref[pl.ds(HALF, HALF)]
    flight["an0"].wait_recv()
    for f in (2, 3):
        flight[(f, 1)] = send(
            rows.at[SLOT["an0"]], SLOT[(f, 1)], ahead if FLOWS[f][1] > 0 else behind
        )
    def returned(f, k):
        _, sign, hops, _ = FLOWS[f]
        total = part[SLOT[(f, k)]]
        if f in B_FLOWS:
            home[("x", f, k)].wait_recv()
            total = total + back[BACK[("x", f, k)]].astype(jnp.float32)
        if k < hops:
            home[(f, k)].wait_recv()
            total = total + back[BACK[(f, k)]].astype(jnp.float32)
        stage[SLOT[(f, k)]] = total.astype(jnp.bfloat16)
        home[(f, k - 1)] = give(SLOT[(f, k)], BACK[(f, k - 1)], behind if sign > 0 else ahead)

    for k in range(1, 5):
        waiting = list(range(*GROUPS[k - 1]))
        for pair in ((4, 5), (0, 1), (2, 3)):
            for f in pair:
                _, sign, hops, _ = FLOWS[f]
                if k > hops:
                    continue
                flight[(f, k)].wait_recv()
                if k < hops:
                    flight[(f, k + 1)] = send(
                        rows.at[SLOT[(f, k)]], SLOT[(f, k + 1)], ahead if sign > 0 else behind
                    )
                if f in B_FLOWS:
                    flight[("x", f, k)] = send(rows.at[SLOT[(f, k)]], SLOT[("x", f, k)], across)
            if waiting and pair != (2, 3):
                if k == 1:
                    flight["bx0"].wait_recv()
                else:
                    for f in B_FLOWS:
                        if pair == (4, 5):
                            flight[("x", f, k - 1)].wait_recv()
                compute(waiting.pop(0))
    for f in B_FLOWS:
        across_back(SLOT[("x", f, 3)], ("x", f, 3))
    returned(1, 3)
    returned(2, 3)
    flight[("x", 4, 4)].wait_recv()
    compute(GROUPS[4][0])
    across_back(SLOT[("x", 4, 4)], ("x", 4, 4))
    returned(3, 4)
    returned(0, 4)
    returned(5, 3)
    for k in (2, 1):
        for f in B_FLOWS:
            across_back(SLOT[("x", f, k)], ("x", f, k))
    across_back(SLOT["bx0"], "bx0")

    returned(4, 4)
    for f in (3, 0, 4):
        returned(f, 3)
    for k in (2, 1):
        for f in (2, 3, 0, 1, 4, 5):
            returned(f, k)

    def gathered(slot, places):
        total = part[slot]
        for place in places:
            home[place].wait_recv()
            total = total + back[BACK[place]].astype(jnp.float32)
        return total

    stage[SLOT["an0"]] = gathered(SLOT["an0"], [(2, 0), (3, 0)]).astype(jnp.bfloat16)
    home["ax0"] = give(SLOT["an0"], BACK["ax0"], across)
    out_ref[pl.ds(HALF, HALF)] = gathered(SLOT["b0"], ["bx0", (4, 0), (5, 0)])
    out_ref[pl.ds(0, HALF)] = gathered(SLOT["a0"], [(0, 0), (1, 0), "ax0"])
    for copy in sent:
        copy.wait_send()


def visit(normed, col, wg, wu, wd):
    vmem = pl.BlockSpec(memory_space=pltpu.VMEM)
    return pl.pallas_call(
        visit_kernel,
        out_shape=jax.ShapeDtypeStruct((2 * HALF, D), jnp.float32),
        in_specs=[vmem] * 5,
        out_specs=vmem,
        scratch_shapes=[
            pltpu.VMEM((SLOTS, HALF, D), jnp.bfloat16),
            pltpu.VMEM((SLOTS, HALF, D), jnp.float32),
            pltpu.VMEM((SLOTS, HALF, D), jnp.bfloat16),
            pltpu.VMEM((BACKS, HALF, D), jnp.bfloat16),
            pltpu.SemaphoreType.DMA((SLOTS,)),
            pltpu.SemaphoreType.DMA((SLOTS,)),
            pltpu.SemaphoreType.DMA((BACKS,)),
            pltpu.SemaphoreType.DMA((BACKS,)),
        ],
        compiler_params=pltpu.CompilerParams(
            collective_id=0, has_side_effects=True, vmem_limit_bytes=60 * 1024 * 1024
        ),
    )(normed, col, wg, wu, wd)


def passed_along(block, axis, distance):
    devices = range(lax.axis_size(axis))
    route = [((i - distance) % len(devices), i) for i in devices]
    return lax.ppermute(block, axis, route)


def body(acts, norm_gain, w_gate, w_up, w_down, routes, gates):
    me = lax.axis_index("expert")
    gain_row = norm_gain[0]
    current = acts[0]
    named = jnp.arange(4 * EXPERTS, dtype=jnp.int32)[:, None, None, None] // EXPERTS
    dense = jnp.sum(jnp.where(routes[None, :, 0] == named, gates[None, :, 0], 0.0), axis=3)
    column = lax.all_to_all(dense, "expert", split_axis=0, concat_axis=0, tiled=True)
    table = np.array(SOURCE, dtype=np.int32)
    turn = 1 - 2 * (lax.axis_index("section") % 2)
    source = (me // RING + table[:, 0]) % 2 * RING + (me % RING - turn * table[:, 1] + RING) % RING
    column = column.reshape(2 * RING, STOPS, 2, HALF).transpose(1, 0, 2, 3)
    column = column.reshape(STOPS, 4 * RING, HALF)
    column = jnp.take(column, source * 2 + table[:, 2], axis=1)[..., None]
    for stop_index in range(STOPS):
        current = passed_along(current, "section", 1)
        widened = current.astype(jnp.float32)
        scale_row = lax.rsqrt(jnp.mean(widened * widened, axis=-1, keepdims=True) + epsilon)
        normed = (widened * scale_row * gain_row).astype(jnp.bfloat16)
        mixture = visit(normed, column[stop_index], w_gate[0], w_up[0], w_down[0])
        current = (widened + mixture).astype(jnp.bfloat16)
    return current[None]


def solution(mesh):
    placed = (
        P("section", ("expert", "dp"), None),
        P("section", None),
        P("section", None, "expert"),
        P("section", None, "expert"),
        P("section", "expert", None),
        P(None, "section", ("expert", "dp"), None),
        P(None, "section", ("expert", "dp"), None),
    )
    return jax.shard_map(
        body,
        mesh=mesh,
        in_specs=placed,
        out_specs=P("section", ("expert", "dp"), None),
        check_vma=False,
    )
```

```python
import jax
import jax.numpy as jnp
import numpy as np
from jax import lax
from jax.experimental import pallas as pl
from jax.experimental.pallas import tpu as pltpu
from jax.sharding import PartitionSpec as P

D = 1536
EXPERTS = 4
STOPS = 2
RING = 8
HALF = 64

epsilon = 1e-05

FLOWS = (
    ("a", 1, 4, 0),
    ("a", -1, 3, 0),
    ("a", 1, 3, 1),
    ("a", -1, 4, 1),
    ("b", 1, 4, 0),
    ("b", -1, 3, 0),
)
B_FLOWS = (4, 5)

SLOT = {"a0": 0, "an0": 1, "b0": 2, "bx0": 3}
SOURCE = [(0, 0, 0), (1, 0, 0), (0, 0, 1), (1, 0, 1)]
GROUPS = [(0, 1)]
for _k in range(1, 5):
    _first = len(SOURCE)
    for _f, (_b, _s, _n, _o) in enumerate(FLOWS):
        if _k <= _n:
            SLOT[(_f, _k)] = len(SOURCE)
            SOURCE.append((_o, _s * _k, int(_b == "b")))
    for _f in B_FLOWS:
        if _k <= FLOWS[_f][2]:
            SLOT[("x", _f, _k)] = len(SOURCE)
            SOURCE.append((1, FLOWS[_f][1] * _k, 1))
    GROUPS.append((_first // 4, len(SOURCE) // 4))
SLOTS = len(SOURCE)

BACK = {}
for _f, _flow in enumerate(FLOWS):
    for _k in range(_flow[2]):
        BACK[(_f, _k)] = len(BACK)
for _f in B_FLOWS:
    for _k in range(1, FLOWS[_f][2] + 1):
        BACK[("x", _f, _k)] = len(BACK)
BACK["bx0"] = len(BACK)
BACK["ax0"] = len(BACK)
BACKS = len(BACK)


def visit_kernel(
    x_ref, moved_ref, col_ref, wg_hbm, wu_hbm, wd_hbm, out_ref,
    rows, part, stage, back, wg_ref, wu_ref, wd_ref,
    send_sem, recv_sem, bsend_sem, brecv_sem, weight_sem,
):
    weights = [
        pltpu.make_async_copy(source, held, weight_sem.at[i])
        for i, (source, held) in enumerate(
            ((wg_hbm, wg_ref), (wu_hbm, wu_ref), (wd_hbm, wd_ref))
        )
    ]
    for copy in weights:
        copy.start()
    me = lax.axis_index("expert")
    ring = me // RING
    y = me % RING
    turn = 1 - 2 * (lax.axis_index("section") % 2)
    ahead = ring * RING + (y + turn + RING) % RING
    behind = ring * RING + (y - turn + RING) % RING
    across = (1 - ring) * RING + y

    barrier = pltpu.get_barrier_semaphore()
    for peer in (ahead, behind, across):
        pl.semaphore_signal(
            barrier, inc=1, device_id={"expert": peer}, device_id_type=pl.DeviceIdType.MESH
        )
    pl.semaphore_wait(barrier, 3)

    own = {"a": x_ref.at[pl.ds(0, HALF)], "b": x_ref.at[pl.ds(HALF, HALF)]}
    sent = []

    def send(source, slot, peer):
        copy = pltpu.make_async_remote_copy(
            src_ref=source,
            dst_ref=rows.at[slot],
            send_sem=send_sem.at[slot],
            recv_sem=recv_sem.at[slot],
            device_id={"expert": peer},
            device_id_type=pl.DeviceIdType.MESH,
        )
        copy.start()
        sent.append(copy)
        return copy

    def give(slot, place, peer):
        copy = pltpu.make_async_remote_copy(
            src_ref=stage.at[slot],
            dst_ref=back.at[place],
            send_sem=bsend_sem.at[place],
            recv_sem=brecv_sem.at[place],
            device_id={"expert": peer},
            device_id_type=pl.DeviceIdType.MESH,
        )
        copy.start()
        sent.append(copy)
        return copy

    def compute(c):
        def chunk(i, carry):
            x = rows[pl.ds(i * 4, 4)].reshape(4 * HALF, D)
            g = jnp.dot(x, wg_ref[...], preferred_element_type=jnp.float32)
            u = jnp.dot(x, wu_ref[...], preferred_element_type=jnp.float32)
            h = (g / (1.0 + jnp.exp(-g)) * u).astype(jnp.bfloat16)
            p = jnp.dot(h, wd_ref[...], preferred_element_type=jnp.float32)
            w = col_ref[pl.ds(i * 4, 4)].reshape(4 * HALF, 1)
            part[pl.ds(i * 4, 4)] = (p * w).reshape(4, HALF, D)
            return carry

        lax.fori_loop(c, c + 1, chunk, 0)

    flight = {}
    home = {}

    def across_back(slot, place):
        stage[slot] = part[slot].astype(jnp.bfloat16)
        home[place] = give(slot, BACK[place], across)

    flight["an0"] = send(own["a"], SLOT["an0"], across)
    for f in (4, 5, 0, 1):
        block, sign, _, _ = FLOWS[f]
        flight[(f, 1)] = send(own[block], SLOT[(f, 1)], ahead if sign > 0 else behind)
    flight["bx0"] = send(own["b"], SLOT["bx0"], across)
    rows[SLOT["a0"]] = x_ref[pl.ds(0, HALF)]
    rows[SLOT["b0"]] = x_ref[pl.ds(HALF, HALF)]
    flight["an0"].wait_recv()
    for f in (2, 3):
        flight[(f, 1)] = send(
            rows.at[SLOT["an0"]], SLOT[(f, 1)], ahead if FLOWS[f][1] > 0 else behind
        )
    def returned(f, k):
        _, sign, hops, _ = FLOWS[f]
        total = part[SLOT[(f, k)]]
        if f in B_FLOWS:
            home[("x", f, k)].wait_recv()
            total = total + back[BACK[("x", f, k)]].astype(jnp.float32)
        if k < hops:
            home[(f, k)].wait_recv()
            total = total + back[BACK[(f, k)]].astype(jnp.float32)
        stage[SLOT[(f, k)]] = total.astype(jnp.bfloat16)
        home[(f, k - 1)] = give(SLOT[(f, k)], BACK[(f, k - 1)], behind if sign > 0 else ahead)

    for copy in weights:
        copy.wait()
    for k in range(1, 5):
        waiting = list(range(*GROUPS[k - 1]))
        for pair in ((4, 5), (0, 1), (2, 3)):
            for f in pair:
                _, sign, hops, _ = FLOWS[f]
                if k > hops:
                    continue
                flight[(f, k)].wait_recv()
                if k < hops:
                    flight[(f, k + 1)] = send(
                        rows.at[SLOT[(f, k)]], SLOT[(f, k + 1)], ahead if sign > 0 else behind
                    )
                if f in B_FLOWS:
                    flight[("x", f, k)] = send(rows.at[SLOT[(f, k)]], SLOT[("x", f, k)], across)
            if waiting and pair != (2, 3):
                if k == 1:
                    flight["bx0"].wait_recv()
                else:
                    for f in B_FLOWS:
                        if pair == (4, 5):
                            flight[("x", f, k - 1)].wait_recv()
                compute(waiting.pop(0))
    for f in B_FLOWS:
        across_back(SLOT[("x", f, 3)], ("x", f, 3))
    returned(1, 3)
    returned(2, 3)
    flight[("x", 4, 4)].wait_recv()
    compute(GROUPS[4][0])
    across_back(SLOT[("x", 4, 4)], ("x", 4, 4))
    returned(3, 4)
    returned(0, 4)
    returned(5, 3)
    for k in (2, 1):
        for f in B_FLOWS:
            across_back(SLOT[("x", f, k)], ("x", f, k))
    across_back(SLOT["bx0"], "bx0")

    returned(4, 4)
    for f in (3, 0, 4):
        returned(f, 3)
    for k in (2, 1):
        for f in (2, 3, 0, 1, 4, 5):
            returned(f, k)

    def gathered(slot, places):
        total = part[slot]
        for place in places:
            home[place].wait_recv()
            total = total + back[BACK[place]].astype(jnp.float32)
        return total

    stage[SLOT["an0"]] = gathered(SLOT["an0"], [(2, 0), (3, 0)]).astype(jnp.bfloat16)
    home["ax0"] = give(SLOT["an0"], BACK["ax0"], across)

    def finish(first, total):
        old = moved_ref[pl.ds(first, HALF)].astype(jnp.float32)
        out_ref[pl.ds(first, HALF)] = (old + total).astype(jnp.bfloat16)

    finish(HALF, gathered(SLOT["b0"], ["bx0", (4, 0), (5, 0)]))
    finish(0, gathered(SLOT["a0"], [(0, 0), (1, 0), "ax0"]))
    for copy in sent:
        copy.wait_send()


def visit(normed, moved, col, wg, wu, wd):
    vmem = pl.BlockSpec(memory_space=pltpu.VMEM)
    return pl.pallas_call(
        visit_kernel,
        out_shape=jax.ShapeDtypeStruct((2 * HALF, D), jnp.bfloat16),
        in_specs=[vmem] * 3 + [pl.BlockSpec(memory_space=pl.ANY)] * 3,
        out_specs=vmem,
        scratch_shapes=[
            pltpu.VMEM((SLOTS, HALF, D), jnp.bfloat16),
            pltpu.VMEM((SLOTS, HALF, D), jnp.float32),
            pltpu.VMEM((SLOTS, HALF, D), jnp.bfloat16),
            pltpu.VMEM((BACKS, HALF, D), jnp.bfloat16),
            pltpu.VMEM(wg.shape, wg.dtype),
            pltpu.VMEM(wu.shape, wu.dtype),
            pltpu.VMEM(wd.shape, wd.dtype),
            pltpu.SemaphoreType.DMA((SLOTS,)),
            pltpu.SemaphoreType.DMA((SLOTS,)),
            pltpu.SemaphoreType.DMA((BACKS,)),
            pltpu.SemaphoreType.DMA((BACKS,)),
            pltpu.SemaphoreType.DMA((3,)),
        ],
        compiler_params=pltpu.CompilerParams(
            collective_id=0, has_side_effects=True, vmem_limit_bytes=60 * 1024 * 1024
        ),
    )(normed, moved, col, wg, wu, wd)


def passed_along(block, axis, distance):
    devices = range(lax.axis_size(axis))
    route = [((i - distance) % len(devices), i) for i in devices]
    return lax.ppermute(block, axis, route)


def body(acts, norm_gain, w_gate, w_up, w_down, routes, gates):
    me = lax.axis_index("expert")
    gain_row = norm_gain[0]
    current = acts[0]
    named = jnp.arange(4 * EXPERTS, dtype=jnp.int32)[:, None, None, None] // EXPERTS
    dense = jnp.sum(jnp.where(routes[None, :, 0] == named, gates[None, :, 0], 0.0), axis=3)
    column = lax.all_to_all(dense, "expert", split_axis=0, concat_axis=0, tiled=True)
    table = np.array(SOURCE, dtype=np.int32)
    turn = 1 - 2 * (lax.axis_index("section") % 2)
    source = (me // RING + table[:, 0]) % 2 * RING + (me % RING - turn * table[:, 1] + RING) % RING
    column = column.reshape(2 * RING, STOPS, 2, HALF).transpose(1, 0, 2, 3)
    column = column.reshape(STOPS, 4 * RING, HALF)
    column = jnp.take(column, source * 2 + table[:, 2], axis=1)[..., None]
    for stop_index in range(STOPS):
        current = passed_along(current, "section", 1)
        widened = current.astype(jnp.float32)
        scale_row = lax.rsqrt(jnp.mean(widened * widened, axis=-1, keepdims=True) + epsilon)
        normed = (widened * scale_row * gain_row).astype(jnp.bfloat16)
        current = visit(
            normed, current, column[stop_index], w_gate[0], w_up[0], w_down[0]
        )
    return current[None]


def solution(mesh):
    placed = (
        P("section", ("expert", "dp"), None),
        P("section", None),
        P("section", None, "expert"),
        P("section", None, "expert"),
        P("section", "expert", None),
        P(None, "section", ("expert", "dp"), None),
        P(None, "section", ("expert", "dp"), None),
    )
    return jax.shard_map(
        body,
        mesh=mesh,
        in_specs=placed,
        out_specs=P("section", ("expert", "dp"), None),
        check_vma=False,
    )
```
